32 devices in a mesh: item: 2 (over x), lat: 4 (over y, core), pix: 4 (over z).
Axes of the slice: x: 2, y: 2, z: 4, core: 2. Of those that a mesh axis runs over, the one named last changes fastest.
Arguments:
- latents: bfloat16 [8, 512, 1024], P('item', ('lat', 'pix')), may hold values from -6 to 6
- pixels: bfloat16 [8, 32768, 261], P('item', ('lat', 'pix')), may hold values from -6 to 6
- size_ids: int32 [8], P('item'), may hold values from 0 to 2, as said below
- cross_gain: float32 [1024], replicated, may hold values from 0.25 to 1.75
- pixel_gain: float32 [261], replicated, may hold values from 0.25 to 1.75
- query_weight: bfloat16 [1024, 1024], replicated, may hold values from -0.1875 to 0.1875
- key_weight: bfloat16 [261, 1024], replicated, may hold values from -0.375 to 0.375
- value_weight: bfloat16 [261, 1024], replicated, may hold values from -0.375 to 0.375
- cross_output: bfloat16 [1024, 1024], replicated, may hold values from -9 to 9
- first_gain: float32 [1024], replicated, may hold values from 0.25 to 1.75
- first_up: bfloat16 [1024, 1024], replicated, may hold values from -0.1875 to 0.1875
- first_down: bfloat16 [1024, 1024], replicated, may hold values from -0.1875 to 0.1875
- self_gain: float32 [1024], replicated, may hold values from 0.25 to 1.75
- self_inputs: bfloat16 [1024, 3072], replicated, may hold values from -0.1875 to 0.1875
- self_output: bfloat16 [1024, 1024], replicated, may hold values from -2.5 to 2.5
- second_gain: float32 [1024], replicated, may hold values from 0.25 to 1.75
- second_up: bfloat16 [1024, 1024], replicated, may hold values from -0.1875 to 0.1875
- second_down: bfloat16 [1024, 1024], replicated, may hold values from -0.1875 to 0.1875
- cotangent: bfloat16 [8, 512, 1024], P('item', ('lat', 'pix')), may hold values from -6 to 6
Outputs:
- latents_out: bfloat16 [8, 512, 1024], P('item', ('lat', 'pix'))
- latent_grad: bfloat16 [8, 512, 1024], P('item', ('lat', 'pix'))
- pixel_grad: bfloat16 [8, 32768, 261], P('item', ('lat', 'pix'))
- query_grad: float32 [1024, 1024], P(('item', 'lat', 'pix'))
- cross_out_grad: float32 [1024, 1024], P(('item', 'lat', 'pix'))
- first_up_grad: float32 [1024, 1024], P(('item', 'lat', 'pix'))
- first_down_grad: float32 [1024, 1024], P(('item', 'lat', 'pix'))
- self_in_grad: float32 [1024, 3072], P(('item', 'lat', 'pix'))
- self_out_grad: float32 [1024, 1024], P(('item', 'lat', 'pix'))
- second_up_grad: float32 [1024, 1024], P(('item', 'lat', 'pix'))
- second_down_grad: float32 [1024, 1024], P(('item', 'lat', 'pix'))
- key_grad: float32 [261, 1024], replicated
- value_grad: float32 [261, 1024], replicated
- cross_gain_grad: float32 [1024], replicated
- pixel_gain_grad: float32 [261], replicated
- first_gain_grad: float32 [1024], replicated
- self_gain_grad: float32 [1024], replicated
- second_gain_grad: float32 [1024], replicated
The draws below stay inside these ranges and needn't reach their ends.
Inputs may be any that keep to these rules, and one draw needn't show every extreme that they name: `size_ids`: each of the sizes 0, 1 and 2 is given to at least one image.
All inputs are finite; a program needn't handle non-finite values.
Results may differ from the reference program's by a relative error of at most 0.025.
Values may be sent and summed in bfloat16 or wider, within the bound.
No kernel may reach another device: no remote copies, remote signals or barrier semaphores. Data moves between devices by JAX's collectives and lax.ppermute only.
A program may use at most 256 MiB of HBM per device.

```python
import math
from functools import partial
import jax
import jax.numpy as jnp
from jax import lax

D = 1024
C = 261
HEADS = 8
HEAD_DIM = 128
LATENTS = 512
ITEMS = 8
PIX = 32768


def draw_size_ids(key, part):
    base = jnp.arange(ITEMS, dtype=jnp.int32) % 3
    return jax.random.permutation(key, base)


def levels(stream_key, shape, split, smallest, top_value):
    def one(axis_at, shards_of):
        steps = jax.random.uniform(jax.random.fold_in(jax.random.fold_in(stream_key, 6), axis_at), (shards_of,), jnp.float32, smallest / len(split), top_value / len(split))
        return jnp.repeat(jnp.exp(steps), shape[axis_at] // shards_of).reshape((-1,) + (1,) * (len(shape) - axis_at - 1))

    loudness = one(*split[0])
    for cut in split[1:]:
        loudness = loudness * one(*cut)
    return loudness


def noise(rng, dims, width, most, pieces=(), held_as=jnp.bfloat16):
    entries = width * jax.random.normal(rng, dims, jnp.float32)
    if pieces:
        entries = entries * levels(rng, dims, pieces, -0.22, 0.18)
    return jnp.clip(entries, -most, most).astype(held_as)


def setup_inputs(seed: int = 0) -> dict:
    key_list = jax.random.split(jax.random.key(seed), 20)
    return {
        "latents": noise(key_list[0], (ITEMS, LATENTS, D), 1.0, 6.0, ((0, 2), (1, 16))),
        "pixels": noise(key_list[1], (ITEMS, PIX, C), 1.0, 6.0, ((0, 2), (1, 16))),
        "size_ids": draw_size_ids(jax.random.fold_in(key_list[19], 71), 0),
        "cross_gain": jnp.clip(1.0 + 0.15 * jax.random.normal(key_list[3], (D,), jnp.float32), 0.25, 1.75),
        "pixel_gain": jnp.clip(1.0 + 0.15 * jax.random.normal(key_list[4], (C,), jnp.float32), 0.25, 1.75),
        "query_weight": noise(key_list[5], (D, D), D ** -0.5, 0.1875),
        "key_weight": noise(key_list[6], (C, D), C ** -0.5, 0.375),
        "value_weight": noise(key_list[7], (C, D), C ** -0.5, 0.375),
        "cross_output": noise(key_list[8], (D, D), 1.5, 9.0),
        "first_gain": jnp.clip(1.0 + 0.15 * jax.random.normal(key_list[9], (D,), jnp.float32), 0.25, 1.75),
        "first_up": noise(key_list[10], (D, D), D ** -0.5, 0.1875),
        "first_down": noise(key_list[11], (D, D), D ** -0.5, 0.1875),
        "self_gain": jnp.clip(1.0 + 0.15 * jax.random.normal(key_list[12], (D,), jnp.float32), 0.25, 1.75),
        "self_inputs": noise(key_list[13], (D, 3 * D), D ** -0.5, 0.1875),
        "self_output": noise(key_list[14], (D, D), (max(1, 3 * D // LATENTS)) ** -0.5, 2.5),
        "second_gain": jnp.clip(1.0 + 0.15 * jax.random.normal(key_list[15], (D,), jnp.float32), 0.25, 1.75),
        "second_up": noise(key_list[16], (D, D), D ** -0.5, 0.1875),
        "second_down": noise(key_list[17], (D, D), D ** -0.5, 0.1875),
        "cotangent": noise(key_list[18], (ITEMS, LATENTS, D), 1.0, 6.0, ((0, 2), (1, 16))),
    }


@jax.custom_vjp
def low(v):
    return lax.optimization_barrier(v.astype(jnp.bfloat16)).astype(jnp.float32)

@jax.custom_vjp
def low_back(v):
    return v

def low_keep(v):
    return (low(v), None)

def low_pass(kept, grad):
    return (grad,)

def back_keep(v):
    return (v, None)

def back_low(kept, grad):
    return (low(grad),)
low.defvjp(low_keep, low_pass)
low_back.defvjp(back_keep, back_low)
epsilon = 1e-05
highest = lax.Precision.HIGHEST

def norm_rows(inputs, gain):
    centred = inputs - lax.optimization_barrier(jnp.mean(inputs, axis=-1, keepdims=True))
    inverse = lax.rsqrt(lax.optimization_barrier(jnp.mean(centred * centred, axis=-1, keepdims=True)) + epsilon)
    return centred * inverse * gain

def activation(inputs):
    return jax.nn.gelu(inputs, approximate=True)

def project(inputs, matrix):
    return jnp.einsum('...d,de->...e', inputs, matrix, precision=highest)

def cross_item(operands, pixel_gain, key_weight, value_weight):
    query_rows, pixel_rows, valid_rows = operands
    normed = low(norm_rows(pixel_rows, pixel_gain))
    pixel_keys = low_back(low(project(normed, key_weight)))
    pixel_values = low_back(low(project(normed, value_weight)))
    scores = low_back(jnp.dot(query_rows, pixel_keys.T, precision=highest) * (1.0 / math.sqrt(D)))
    powered = jnp.where(valid_rows[None, :], jnp.exp(scores), 0.0)
    totals = lax.optimization_barrier(jnp.sum(powered, axis=1, keepdims=True))
    numerator = low_back(jnp.dot(low(powered), pixel_values, precision=highest))
    return numerator / totals

def forward(latents, pixels, valid, cross_gain, pixel_gain, query_weight, key_weight, value_weight, cross_output, first_gain, first_up, first_down, self_gain, self_inputs, self_output, second_gain, second_up, second_down):
    images = latents.shape[0]
    normed_one = low(norm_rows(latents, cross_gain))
    cross_query = low_back(low(project(normed_one, query_weight)))
    item_step = jax.checkpoint(partial(cross_item, pixel_gain=pixel_gain, key_weight=key_weight, value_weight=value_weight))
    attended = lax.map(item_step, (cross_query, pixels, valid))
    cross_mixed = low_back(low(attended))
    residual_one = latents + low_back(project(cross_mixed, cross_output))
    normed_two = low(norm_rows(residual_one, first_gain))
    hidden_one = low_back(project(normed_two, first_up))
    residual_two = residual_one + low_back(project(low(activation(hidden_one)), first_down))
    normed_three = low(norm_rows(residual_two, self_gain))
    projected = low_back(low(project(normed_three, self_inputs)))
    head_shape = (images, LATENTS, HEADS, HEAD_DIM)
    self_query = projected[..., :D].reshape(head_shape)
    self_keys = projected[..., D:2 * D].reshape(head_shape)
    self_values = projected[..., 2 * D:].reshape(head_shape)
    self_scores = low_back(jnp.einsum('ilhe,imhe->ihlm', self_query, self_keys, precision=highest) * (1.0 / math.sqrt(HEAD_DIM)))
    self_powered = jnp.exp(self_scores)
    self_totals = lax.optimization_barrier(jnp.sum(self_powered, axis=3))
    self_numerator = low_back(jnp.einsum('ihlm,imhe->ilhe', low(self_powered), self_values, precision=highest))
    self_mixed = self_numerator / jnp.transpose(self_totals, (0, 2, 1))[..., None]
    self_rounded = low_back(low(self_mixed.reshape(images, LATENTS, D)))
    residual_three = residual_two + low_back(project(self_rounded, self_output))
    normed_four = low(norm_rows(residual_three, second_gain))
    hidden_two = low_back(project(normed_four, second_up))
    return residual_three + low_back(project(low(activation(hidden_two)), second_down))

def reference(latents, pixels, size_ids, cross_gain, pixel_gain, query_weight, key_weight, value_weight, cross_output, first_gain, first_up, first_down, self_gain, self_inputs, self_output, second_gain, second_up, second_down, cotangent):
    factor = jnp.where(size_ids == 0, 25, jnp.where(size_ids == 1, 49, 81)).astype(jnp.int32)
    counts = PIX * factor // 81
    valid = jnp.arange(PIX, dtype=jnp.int32)[None, :] < counts[:, None]
    floats = tuple((array.astype(jnp.float32) for array in (latents, pixels, cross_gain, pixel_gain, query_weight, key_weight, value_weight, cross_output, first_gain, first_up, first_down, self_gain, self_inputs, self_output, second_gain, second_up, second_down)))

    def closed(latent_in, pixel_in, *params):
        return forward(latent_in, pixel_in, valid, *params)
    result, pullback = jax.vjp(closed, *floats)
    latent_grad, pixel_grad, cross_gain_grad, pixel_gain_grad, query_grad, key_grad, value_grad, cross_out_grad, first_gain_grad, first_up_grad, first_down_grad, self_gain_grad, self_in_grad, self_out_grad, second_gain_grad, second_up_grad, second_down_grad = pullback(cotangent.astype(jnp.float32))
    return (result.astype(jnp.bfloat16), latent_grad.astype(jnp.bfloat16), pixel_grad.astype(jnp.bfloat16), query_grad, cross_out_grad, first_up_grad, first_down_grad, self_in_grad, self_out_grad, second_up_grad, second_down_grad, key_grad, value_grad, cross_gain_grad, pixel_gain_grad, first_gain_grad, self_gain_grad, second_gain_grad)
```

```python
import math
from functools import partial

import jax
import jax.numpy as jnp
from jax import lax
from jax.experimental import pallas as pl
from jax.experimental.pallas import tpu as pltpu
from jax.sharding import Mesh, PartitionSpec as P

HEADS = 8
LANES = 128
epsilon = 1e-05
f32 = jnp.float32
bf16 = jnp.bfloat16

NN = (((1,), (0,)), ((), ()))
NT = (((1,), (1,)), ((), ()))
TN = (((0,), (0,)), ((), ()))


def dot(left, right, dims=NN):
    return lax.dot_general(left, right, dims, preferred_element_type=f32)


def norm_rows(inputs, gain):
    centred = inputs - jnp.mean(inputs, axis=-1, keepdims=True)
    inverse = lax.rsqrt(jnp.mean(centred * centred, axis=-1, keepdims=True) + epsilon)
    normed = centred * inverse
    return (normed * gain, normed, inverse)


def norm_back(upstream, normed, inverse, gain):
    scaled = upstream * gain
    first_mean = jnp.mean(scaled, axis=-1, keepdims=True)
    second_mean = jnp.mean(scaled * normed, axis=-1, keepdims=True)
    return inverse * (scaled - first_mean - normed * second_mean)


def activation(inputs):
    return jax.nn.gelu(inputs, approximate=True)


def pixel_norm(x_ref, channels):
    raw = x_ref[0].astype(f32)
    rows, padded = raw.shape
    lane = lax.broadcasted_iota(jnp.int32, (rows, padded), 1)
    inside = lane < channels
    raw = jnp.where(inside, raw, 0.0)
    mean = jnp.sum(raw, axis=1, keepdims=True) * (1.0 / channels)
    centred = jnp.where(inside, raw - mean, 0.0)
    inverse = lax.rsqrt(
        jnp.sum(centred * centred, axis=1, keepdims=True) * (1.0 / channels) + epsilon
    )
    return centred * inverse, inverse, lane, inside


def rounded_pixels(normed, gain, lane, channels):
    ones = jnp.where((lane >= channels) & (lane < channels + 2), 1.0, 0.0)
    return (normed * gain + ones).astype(bf16)


def both_halves(a_ref, b_ref, padded):
    rows = math.prod(a_ref.shape) // padded
    return jnp.concatenate(
        [a_ref[...].reshape(rows, padded), b_ref[...].reshape(rows, padded)], axis=0
    )


def cross_forward_kernel(
    counts_ref, x_ref, gain_ref, qa_ref, qb_ref, p_ref, na_ref, nb_ref, acc_ref, *, channels, tile
):
    image, step = pl.program_id(0), pl.program_id(1)
    padded = x_ref.shape[2]

    @pl.when(step == 0)
    def _():
        acc_ref[...] = jnp.zeros_like(acc_ref)

    left = counts_ref[image] - step * tile

    @pl.when(left > 0)
    def _():
        normed, _, lane, _ = pixel_norm(x_ref, channels)
        pixels = rounded_pixels(normed, gain_ref[...], lane, channels)
        queries = both_halves(qa_ref, qb_ref, padded)
        scores = dot(pixels, queries, NT)
        row = lax.broadcasted_iota(jnp.int32, scores.shape, 0)
        powered = jnp.where(row < left, jnp.exp(scores), 0.0).astype(bf16)
        p_ref[0] = powered
        acc_ref[...] += dot(powered, pixels, TN)

    @pl.when(step == pl.num_programs(1) - 1)
    def _():
        half = acc_ref.shape[0] // 2
        na_ref[...] = acc_ref[:half].reshape(na_ref.shape).astype(bf16)
        nb_ref[...] = acc_ref[half:].reshape(nb_ref.shape).astype(bf16)


def cross_backward_kernel(
    counts_ref,
    x_ref,
    gain_ref,
    qa_ref,
    qb_ref,
    ga_ref,
    gb_ref,
    p_ref,
    out_ref,
    ta_ref,
    tb_ref,
    acc_ref,
    *,
    channels,
    tile,
):
    image, step = pl.program_id(0), pl.program_id(1)
    padded = x_ref.shape[2]

    @pl.when(step == 0)
    def _():
        acc_ref[...] = jnp.zeros_like(acc_ref)

    left = counts_ref[image] - step * tile

    @pl.when(left > 0)
    def _():
        gain = gain_ref[...]
        normed, inverse, lane, inside = pixel_norm(x_ref, channels)
        pixels = rounded_pixels(normed, gain, lane, channels)
        queries = both_halves(qa_ref, qb_ref, padded)
        grads = both_halves(ga_ref, gb_ref, padded)
        powered = p_ref[0]
        power_grad = dot(pixels, grads, NT)
        score_grad = (powered.astype(f32) * power_grad).astype(bf16)
        acc_ref[...] += dot(score_grad, pixels, TN)
        upstream = dot(score_grad, queries) + dot(powered, grads)
        scaled = jnp.where(inside, upstream * gain, 0.0)
        first_mean = jnp.sum(scaled, axis=1, keepdims=True) * (1.0 / channels)
        second_mean = jnp.sum(scaled * normed, axis=1, keepdims=True) * (1.0 / channels)
        out_ref[0] = (inverse * (scaled - first_mean - normed * second_mean)).astype(bf16)

    @pl.when(left <= 0)
    def _():
        out_ref[...] = jnp.zeros_like(out_ref)

    @pl.when(step == pl.num_programs(1) - 1)
    def _():
        half = acc_ref.shape[0] // 2
        ta_ref[...] = acc_ref[:half].reshape(ta_ref.shape).astype(bf16)
        tb_ref[...] = acc_ref[half:].reshape(tb_ref.shape).astype(bf16)


def cross_specs(images, pix_rows, padded, tile, fine, share):
    pixel = pl.BlockSpec((1, tile, padded), lambda i, s, c: (i, s, 0))
    gain = pl.BlockSpec((1, padded), lambda i, s, c: (0, 0))
    outer, rows = fine
    latent = pl.BlockSpec((outer, 1, rows, padded), lambda i, s, c: (0, i, 0, 0))
    gathered = pl.BlockSpec((outer, 1, rows, padded), lambda i, s, c: (0, i, 0, 0))
    shared = pl.BlockSpec((share[0], 1, share[1], padded), lambda i, s, c: (0, i, 0, 0))
    return pixel, gain, latent, gathered, shared


PIXEL_TILE = 512


def cross_forward(counts, pixels, gain, qa, qb, image_rows):
    images, pix_rows, channels = pixels.shape
    sources, _, rows, padded = qa.shape
    latents = 2 * sources * rows
    tile = min(PIXEL_TILE, pix_rows)
    steps = pix_rows // tile
    outer = sources * rows // image_rows
    query = pl.BlockSpec((sources, 1, rows, padded), lambda i, s, c: (0, i, 0, 0))
    numer = pl.BlockSpec((outer, 1, image_rows, padded), lambda i, s, c: (0, i, 0, 0))
    numer_shape = jax.ShapeDtypeStruct((outer, images, image_rows, padded), bf16)
    flops = 2 * 2 * images * latents * pix_rows * padded
    return pl.pallas_call(
        partial(cross_forward_kernel, channels=channels, tile=tile),
        grid_spec=pltpu.PrefetchScalarGridSpec(
            num_scalar_prefetch=1,
            grid=(images, steps),
            in_specs=[
                pl.BlockSpec((1, tile, padded), lambda i, s, c: (i, s, 0)),
                pl.BlockSpec((1, padded), lambda i, s, c: (0, 0)),
                query,
                query,
            ],
            out_specs=[
                pl.BlockSpec((1, tile, latents), lambda i, s, c: (i, s, 0)),
                numer,
                numer,
            ],
            scratch_shapes=[pltpu.VMEM((latents, padded), f32)],
        ),
        out_shape=[
            jax.ShapeDtypeStruct((images, pix_rows, latents), bf16),
            numer_shape,
            numer_shape,
        ],
        compiler_params=pltpu.CompilerParams(dimension_semantics=("arbitrary", "arbitrary")),
        cost_estimate=pl.CostEstimate(
            flops=flops,
            bytes_accessed=2 * images * pix_rows * (padded + latents),
            transcendentals=images * pix_rows * latents,
        ),
        name="cross_forward",
    )(counts, pixels, gain, qa, qb)


def cross_backward(counts, pixels, gain, qa, qb, ga, gb, powered):
    images, pix_rows, channels = pixels.shape
    sources, _, rows, padded = qa.shape
    outer, _, image_rows, _ = ga.shape
    latents = 2 * sources * rows
    tile = min(PIXEL_TILE, pix_rows)
    steps = pix_rows // tile
    query = pl.BlockSpec((sources, 1, rows, padded), lambda i, s, c: (0, i, 0, 0))
    grad = pl.BlockSpec((outer, 1, image_rows, padded), lambda i, s, c: (0, i, 0, 0))
    pixel = pl.BlockSpec((1, tile, padded), lambda i, s, c: (i, s, 0))
    t_shape = jax.ShapeDtypeStruct((sources, images, rows, padded), bf16)
    flops = 2 * 4 * images * latents * pix_rows * padded
    return pl.pallas_call(
        partial(cross_backward_kernel, channels=channels, tile=tile),
        grid_spec=pltpu.PrefetchScalarGridSpec(
            num_scalar_prefetch=1,
            grid=(images, steps),
            in_specs=[
                pixel,
                pl.BlockSpec((1, padded), lambda i, s, c: (0, 0)),
                query,
                query,
                grad,
                grad,
                pl.BlockSpec((1, tile, latents), lambda i, s, c: (i, s, 0)),
            ],
            out_specs=[pixel, query, query],
            scratch_shapes=[pltpu.VMEM((latents, padded), f32)],
        ),
        out_shape=[jax.ShapeDtypeStruct(pixels.shape, bf16), t_shape, t_shape],
        compiler_params=pltpu.CompilerParams(dimension_semantics=("arbitrary", "arbitrary")),
        cost_estimate=pl.CostEstimate(
            flops=flops,
            bytes_accessed=2 * images * pix_rows * (2 * padded + latents),
            transcendentals=0,
        ),
        name="cross_backward",
    )(counts, pixels, gain, qa, qb, ga, gb, powered)


def self_forward_kernel(q_ref, kv_refs, out_ref, *, head_scale):
    width = q_ref.shape[1]
    dim = width // HEADS
    for head in range(HEADS):
        cut = slice(head * dim, (head + 1) * dim)
        over = slice(width + head * dim, width + (head + 1) * dim)
        query = q_ref[:, cut]
        keys = jnp.concatenate([ref[:, cut] for ref in kv_refs], axis=0)
        values = jnp.concatenate([ref[:, over] for ref in kv_refs], axis=0)
        powered = jnp.exp(dot(query, keys, NT) * head_scale)
        totals = jnp.sum(powered, axis=1, keepdims=True)
        out_ref[:, cut] = (dot(powered.astype(bf16), values) / totals).astype(bf16)


def self_forward(query, parts, head_scale):
    count = len(parts)

    def kernel(*refs):
        self_forward_kernel(refs[0], refs[1 : 1 + count], refs[1 + count], head_scale=head_scale)

    return pl.pallas_call(
        kernel, out_shape=jax.ShapeDtypeStruct(query.shape, bf16), name="self_forward"
    )(query, *parts)


def self_backward_kernel(q_ref, g_ref, kv_refs, dq_ref, dkv_refs, *, head_scale):
    rows, width = q_ref.shape
    dim = width // HEADS
    for head in range(HEADS):
        cut = slice(head * dim, (head + 1) * dim)
        over = slice(width + head * dim, width + (head + 1) * dim)
        query = q_ref[:, cut]
        upstream = g_ref[:, cut].astype(f32)
        keys = jnp.concatenate([ref[:, cut] for ref in kv_refs], axis=0)
        values = jnp.concatenate([ref[:, over] for ref in kv_refs], axis=0)
        powered = jnp.exp(dot(query, keys, NT) * head_scale)
        low = powered.astype(bf16)
        totals = jnp.sum(powered, axis=1, keepdims=True)
        mixed = dot(low, values) / totals
        numer_grad = (upstream / totals).astype(bf16)
        total_grad = -jnp.sum(upstream * mixed, axis=1, keepdims=True) / totals
        score_grad = (powered * (dot(numer_grad, values, NT) + total_grad)).astype(bf16)
        dq_ref[:, cut] = (dot(score_grad, keys) * head_scale).astype(bf16)
        key_grad = (dot(score_grad, query, TN) * head_scale).astype(bf16)
        value_grad = dot(low, numer_grad, TN).astype(bf16)
        for at, ref in enumerate(dkv_refs):
            ref[:, cut] = key_grad[at * rows : (at + 1) * rows]
            ref[:, over] = value_grad[at * rows : (at + 1) * rows]


def self_backward(query, upstream, parts, head_scale):
    count = len(parts)

    def kernel(*refs):
        self_backward_kernel(
            refs[0],
            refs[1],
            refs[2 : 2 + count],
            refs[2 + count],
            refs[3 + count :],
            head_scale=head_scale,
        )

    return pl.pallas_call(
        kernel,
        out_shape=[jax.ShapeDtypeStruct(query.shape, bf16)]
        + [jax.ShapeDtypeStruct(part.shape, bf16) for part in parts],
        name="self_backward",
    )(query, upstream, *parts)


def swap(value, axis):
    return lax.ppermute(value, axis, [(0, 1), (1, 0)])


def pix_exchange(value):
    size = lax.axis_size("pix")
    me = lax.axis_index("pix")
    out = value
    for step in range(1, size):
        perm = [(at, at ^ step) for at in range(size)]
        peer = me ^ step
        got = lax.ppermute(lax.dynamic_index_in_dim(value, peer, 0, keepdims=True), "pix", perm)
        out = lax.dynamic_update_slice_in_dim(out, got, peer, 0)
    return out


GRID = ("laty", "pix")
EVERY = ("item", "laty", "pix")


def spread(value, axes):
    size = lax.axis_size(axes)
    many = jnp.broadcast_to(value[None], (size,) + value.shape)
    return lax.all_to_all(many, axes, split_axis=0, concat_axis=0, tiled=True)


def pair_sum(mine, theirs):
    return (mine.astype(f32) + swap(theirs, "latc").astype(f32)).astype(bf16)


def collect(value, axes):
    got = lax.all_to_all(value, axes, split_axis=0, concat_axis=0, tiled=True)
    size = lax.axis_size(axes)
    got = got.reshape((size, value.shape[0] // size) + value.shape[1:])
    return jnp.sum(got.astype(f32), axis=0)


def body(
    latents,
    pixels,
    size_ids,
    cross_gain,
    pixel_gain,
    query_weight,
    key_weight,
    value_weight,
    cross_output,
    first_gain,
    first_up,
    first_down,
    self_gain,
    self_inputs,
    self_output,
    second_gain,
    second_up,
    second_down,
    cotangent,
):
    images, lat_rows, width = latents.shape
    pix_rows, channels = pixels.shape[1:]
    padded = -(-(channels + 2) // LANES) * LANES
    head_scale = 1.0 / math.sqrt(width // HEADS)
    scale = 1.0 / math.sqrt(width)
    items, laty, latc, pix = (lax.axis_size(a) for a in ("item", "laty", "latc", "pix"))
    assert images == pix and latc == 2 and laty == 2
    group = laty * latc * pix
    grid = laty * pix
    rows = images * lat_rows
    core = lax.axis_index("latc")
    block = lax.axis_index(("laty", "latc", "pix"))
    factor = jnp.where(size_ids == 0, 25, jnp.where(size_ids == 1, 49, 81)).astype(jnp.int32)
    counts = pix_rows * group * factor // 81
    counts = jnp.clip(counts - block * pix_rows, 0, pix_rows)
    lanes = ((0, padded - channels),)
    key_pad = jnp.pad(key_weight, lanes + ((0, 0),))
    value_pad = jnp.pad(value_weight, lanes + ((0, 0),))
    gain_pad = jnp.pad(pixel_gain, lanes)[None]

    latents_here = latents.astype(f32).reshape(rows, width)
    normed_full, normed_one, inverse_one = norm_rows(latents_here, cross_gain)
    rounded_one = normed_full.astype(bf16)
    query_rows = dot(rounded_one, query_weight).astype(bf16)
    query_low = (dot(query_rows, key_pad, NT) * scale).astype(bf16)
    qa = spread(query_low.reshape(images, lat_rows, padded), GRID)
    qb = swap(qa, "latc")
    powered, numer_a, numer_b = cross_forward(counts, pixels, gain_pad, qa, qb, pix * lat_rows)

    residual_zero = pix_exchange(latents).astype(f32).reshape(rows, width)
    upstream = pix_exchange(cotangent).reshape(rows, width)
    numer = collect(
        pair_sum(numer_a, numer_b).reshape(grid, rows, padded), GRID
    ).reshape(rows, padded)
    totals = numer[:, channels : channels + 1]
    numer_mean = (numer / totals).astype(bf16)
    attended = dot(numer_mean, value_pad)
    cross_mixed = attended.astype(bf16)
    residual_one = residual_zero + dot(cross_mixed, cross_output)

    def feed_forward(residual, gain, up_weight, down_weight):
        normed_full, normed, inverse = norm_rows(residual, gain)
        rounded_in = normed_full.astype(bf16)
        hidden = dot(rounded_in, up_weight)
        active = activation(hidden).astype(bf16)
        return residual + dot(active, down_weight), (rounded_in, normed, inverse, hidden, active)

    def shared_left(left):
        parts = left.reshape(rows, items * laty, 2, -1)
        mine = lax.dynamic_index_in_dim(parts, core, 2, keepdims=False)
        theirs = lax.dynamic_index_in_dim(parts, 1 - core, 2, keepdims=False)
        return jnp.concatenate([mine, swap(theirs, "latc")], axis=0).reshape(2 * rows, -1)

    def shared_right(right):
        return jnp.concatenate([right, swap(right, "latc")], axis=0)

    def weight_grad(left, right):
        grad = dot(shared_left(left), shared_right(right), TN).astype(bf16)
        return grad.reshape(items * grid, -1, right.shape[1])

    def scatter(grads):
        whole = jnp.concatenate(grads, axis=2)
        for axis in EVERY:
            whole = lax.psum_scatter(whole, axis, scatter_dimension=0, tiled=True)
        whole = whole[0].astype(f32)
        out, at = [], 0
        for grad in grads:
            out.append(whole[:, at : at + grad.shape[2]])
            at += grad.shape[2]
        return out

    residual_two, first_kept = feed_forward(residual_one, first_gain, first_up, first_down)
    normed_full, normed_three, inverse_three = norm_rows(residual_two, self_gain)
    rounded_three = normed_full.astype(bf16)
    projected = dot(rounded_three, self_inputs).astype(bf16)
    self_query = projected[:, :width]
    pair = projected[:, width:]
    pair_y = swap(pair, "laty")
    parts = (pair, pair_y, swap(pair, "latc"), swap(pair_y, "latc"))
    self_rounded = self_forward(self_query, parts, head_scale)
    residual_three = residual_two + dot(self_rounded, self_output)
    output_rows, second_kept = feed_forward(residual_three, second_gain, second_up, second_down)
    latents_out = pix_exchange(output_rows.astype(bf16).reshape(images, lat_rows, width))

    def feed_back(upstream, kept, gain, up_weight, down_weight):
        rounded_in, normed, inverse, hidden, active = kept
        sent = upstream.astype(bf16)
        down_grad = weight_grad(active, sent)
        _, gelu_pull = jax.vjp(activation, hidden)
        hidden_grad = gelu_pull(dot(sent, down_weight, NT))[0].astype(bf16)
        up_grad = weight_grad(rounded_in, hidden_grad)
        normed_grad = dot(hidden_grad, up_weight, NT)
        gain_grad = jnp.sum(normed_grad * normed, axis=0)
        return (
            upstream.astype(f32) + norm_back(normed_grad, normed, inverse, gain),
            up_grad,
            down_grad,
            gain_grad,
        )

    back_three, second_up_part, second_down_part, second_gain_part = feed_back(
        upstream, second_kept, second_gain, second_up, second_down
    )
    sent_three = back_three.astype(bf16)
    self_out_part = weight_grad(self_rounded, sent_three)
    second_up_grad, second_down_grad, self_out_grad = scatter(
        [second_up_part, second_down_part, self_out_part]
    )
    mixed_grad = dot(sent_three, self_output, NT).astype(bf16)
    query_part, own, at_y, at_c, at_yc = self_backward(self_query, mixed_grad, parts, head_scale)
    near = pair_sum(own, at_c)
    far = pair_sum(at_y, at_yc)
    pair_own = (near.astype(f32) + swap(far, "laty").astype(f32)).astype(bf16)
    projected_grad = jnp.concatenate([query_part, pair_own], axis=1)
    self_in_part = weight_grad(rounded_three, projected_grad)
    normed_grad = dot(projected_grad, self_inputs, NT)
    self_gain_part = jnp.sum(normed_grad * normed_three, axis=0)
    back_two = back_three + norm_back(normed_grad, normed_three, inverse_three, self_gain)
    back_one, first_up_part, first_down_part, first_gain_part = feed_back(
        back_two, first_kept, first_gain, first_up, first_down
    )
    self_in_grad, first_up_grad, first_down_grad = scatter(
        [self_in_part, first_up_part, first_down_part]
    )
    sent_one = back_one.astype(bf16)
    attended_grad = dot(sent_one, cross_output, NT).astype(bf16).astype(f32)
    numer_grad = (attended_grad / totals).astype(bf16)
    total_grad = -jnp.sum(attended_grad * attended, axis=1, keepdims=True) / totals
    lane = lax.broadcasted_iota(jnp.int32, (rows, padded), 1)
    high = total_grad.astype(bf16).astype(f32)
    grad_low = dot(numer_grad, value_pad, NT)
    grad_low = jnp.where(lane == channels, high, grad_low)
    grad_low = jnp.where(lane == channels + 1, total_grad - high, grad_low).astype(bf16)
    ga = spread(grad_low, GRID).reshape(laty, images, rows, padded)
    gb = swap(ga, "latc")
    pixel_grad, t_a, t_b = cross_backward(counts, pixels, gain_pad, qa, qb, ga, gb, powered)
    back_here = pix_exchange(sent_one.reshape(images, lat_rows, width))
    t_rows = collect(pair_sum(t_a, t_b), GRID).reshape(rows, padded)
    t_low = (t_rows * scale).astype(bf16)
    query_rows_grad = dot(t_low, key_pad).astype(bf16)
    normed_one_grad = dot(query_rows_grad, query_weight, NT)
    latent_grad = back_here.astype(f32).reshape(rows, width) + norm_back(
        normed_one_grad, normed_one, inverse_one, cross_gain
    )
    latent_grad = latent_grad.astype(bf16).reshape(images, lat_rows, width)

    first_sum = dot(rounded_one, t_low, TN)
    second_sum = dot(sent_one, numer_mean, TN)
    wide = lax.broadcasted_iota(jnp.int32, (width, padded), 1)
    for at, part in enumerate((first_gain_part, self_gain_part, second_gain_part)):
        column = channels + 2 * at
        part = part[:, None]
        high = part.astype(bf16).astype(f32)
        first_sum = jnp.where(wide == column, high, first_sum)
        first_sum = jnp.where(wide == column + 1, part - high, first_sum)
    sums = jnp.stack([first_sum, second_sum]).astype(bf16)
    sums = sums.reshape(2, items, laty, 2, pix, -1, padded).transpose(3, 1, 2, 4, 0, 5, 6)
    sums = sums.reshape((2, items * grid) + sums.shape[4:])
    mine = lax.dynamic_index_in_dim(sums, core, 0, keepdims=False)
    theirs = lax.dynamic_index_in_dim(sums, 1 - core, 0, keepdims=False)
    owned = collect(pair_sum(mine, theirs), EVERY)[0].astype(bf16)
    mine = spread(owned, EVERY)
    theirs = swap(mine, "latc")
    low = jnp.where(core == 0, mine, theirs)
    high = jnp.where(core == 0, theirs, mine)
    sums = jnp.stack([low, high]).reshape((2, items, laty, pix) + owned.shape)
    sums = sums.transpose(4, 1, 2, 0, 3, 5, 6).reshape(2, width, padded)
    first_sum, second_sum = sums[0], sums[1]
    gains = [
        first_sum[:, channels + 2 * at].astype(f32) + first_sum[:, channels + 2 * at + 1].astype(f32)
        for at in range(3)
    ]
    first_gain_grad, self_gain_grad, second_gain_grad = gains
    clean = jnp.where(wide < channels, first_sum, 0).astype(bf16)
    query_grad = dot(owned[0], key_pad)
    key_grad = dot(clean, query_weight, TN)[:channels]
    weights = dot(query_weight, key_pad, NT)
    cross_gain_grad = jnp.sum(clean.astype(f32) * weights, axis=1) / cross_gain
    value_grad = dot(second_sum, cross_output, (((0,), (1,)), ((), ())))[:channels]
    start = (lax.axis_index(("item", "laty", "latc", "pix"))) * owned.shape[1]
    columns = lax.dynamic_slice_in_dim(value_pad, start, owned.shape[1], 1)
    cross_out_grad = dot(columns, second_sum, (((0,), (1,)), ((), ())))
    pixel_gain_grad = (
        jnp.sum(
            key_grad * key_weight.astype(f32) + value_grad * value_weight.astype(f32), axis=1
        )
        / pixel_gain
    )
    return (
        latents_out,
        latent_grad,
        pixel_grad,
        query_grad,
        cross_out_grad,
        first_up_grad,
        first_down_grad,
        self_in_grad,
        self_out_grad,
        second_up_grad,
        second_down_grad,
        key_grad,
        value_grad,
        cross_gain_grad,
        pixel_gain_grad,
        first_gain_grad,
        self_gain_grad,
        second_gain_grad,
    )


def solution(mesh):
    items, lat, pix = (mesh.shape[name] for name in ("item", "lat", "pix"))
    fine = Mesh(
        mesh.devices.reshape(items, lat // 2, 2, pix), ("item", "laty", "latc", "pix")
    )
    group = ("laty", "latc", "pix")
    rows = P("item", group, None)
    split = P(("item",) + group, None)
    in_specs = (rows, rows, P("item")) + (P(),) * 15 + (rows,)
    out_specs = (rows, rows, rows) + (split,) * 8 + (P(),) * 7
    return jax.shard_map(
        body, mesh=fine, in_specs=in_specs, out_specs=out_specs, check_vma=False
    )
```
